32 devices in a mesh: members: 2 (over y), lat: 4 (over z), lon: 2 (over x), lev: 2 (over core).
Axes of the slice: x: 2, y: 2, z: 4, core: 2. Of those that a mesh axis runs over, the one named last changes fastest.
Arguments:
- wind_east: float32 [8, 360, 2880], P(('members', 'lev'), 'lat', 'lon'), parts along dimension 0, may hold values from -6 to 6
- wind_north: float32 [8, 360, 2880], P(('members', 'lev'), 'lat', 'lon'), parts along dimension 0, may hold values from -6 to 6
- thickness: float32 [8, 360, 2880], P(('members', 'lev'), 'lat', 'lon'), parts along dimension 0, may hold values from -6 to 6
- geopot: float32 [8, 360, 2880], P(('members', 'lev'), 'lat', 'lon'), parts along dimension 0, may hold values from -6 to 6
- surface_geopot: float32 [360, 2880], P('lat', 'lon'), may hold values from -6 to 6
- mean_depth: float32 [4], P('lev'), may hold values from 0.5 to 2
- kept_modes: int32 [180], replicated, may hold values from 1 to 360
- slot_table: int32 [180], replicated, may hold values from 0 to 179, as said below
Outputs:
- east_final: float32 [8, 360, 2880], P(('members', 'lev'), 'lat', 'lon'), parts along dimension 0
- north_final: float32 [8, 360, 2880], P(('members', 'lev'), 'lat', 'lon'), parts along dimension 0
- thick_new: float32 [8, 360, 2880], P(('members', 'lev'), 'lat', 'lon'), parts along dimension 0
- geo_new: float32 [8, 360, 2880], P(('members', 'lev'), 'lat', 'lon'), parts along dimension 0
- spectra: float32 [2, 8, 180, 720], P(None, ('members', 'lev'), 'lat', 'lon'), parts along dimension 1
The draws below stay inside these ranges and needn't reach their ends.
There are 2 independent parts, one for each index of `members`. The reference program is written for one: setup_inputs(seed, part) draws one part's arguments, and reference() takes and returns one part's arrays. A program takes and returns all parts, laid end to end along the dimension named above; an argument that names none is the same for every part. Nothing has to cross between parts.
Inputs may be any that keep to these rules, and one draw needn't show every extreme that they name: `slot_table`: every slot 0 to 179 is named once; slot s belongs to latitude device s // 45. Of the 90 polar rows held by latitude device d, 45 name slots of device d and 45 name slots of the device half the lat axis away, (d + 4 / 2) mod 4.
All inputs are finite; a program needn't handle non-finite values.
Results may differ from the reference program's by a relative error of at most 0.00019.
Values sent between devices are 32-bit elements; how exact they have to be, the bound alone decides.
A program may use at most 64 MiB of HBM per device.

```python
import math
import jax
import jax.numpy as jnp

NLON = 2880
KMAX = 360
LAT_DEV = 90
NLAT = 360
LEVELS = 4
NP = 90
HELP = 45


def draw_kept_modes(key, part):
    row_rank = jnp.arange(2 * NP, dtype=jnp.int32)
    from_pole = jnp.where(row_rank < NP, row_rank, 2 * NP - 1 - row_rank)
    ramp_value = 1 + (KMAX - 1) * from_pole // (NP - 1)
    jitter_span = max(1, KMAX // 16)
    jitter = jax.random.randint(jax.random.fold_in(key, 7), (2 * NP,), -jitter_span, jitter_span + 1)
    kept_count = jnp.clip(ramp_value + jitter, 1, KMAX)
    kept_count = jnp.where(from_pole == NP - 1, KMAX, kept_count)
    kept_count = jnp.where(from_pole == 0, 1, kept_count)
    return kept_count.astype(jnp.int32)


def draw_slot_table(key, part):
    lat_devices = NLAT // LAT_DEV
    owners = 2 * NP // LAT_DEV
    split_keys = jax.random.split(jax.random.fold_in(key, 12), owners)
    row_ranks = jax.vmap(lambda one_key: jax.random.permutation(one_key, LAT_DEV))(split_keys)
    row_ranks = row_ranks.reshape(-1).astype(jnp.int32)
    owner_block = jnp.arange(2 * NP, dtype=jnp.int32) // LAT_DEV
    owner_device = jnp.where(owner_block < lat_devices // 4, owner_block, owner_block + lat_devices // 2)
    partner_device = (owner_device + lat_devices // 2) % lat_devices
    target_device = jnp.where(row_ranks < HELP, owner_device, partner_device)
    position = row_ranks % HELP
    return (target_device * HELP + position).astype(jnp.int32)


def levels(own_key, shape, cuts, least, top_value):
    gain, own = 1.0, jax.random.fold_in(own_key, 6)
    for dim, parts in cuts:
        draws = jnp.exp(jax.random.uniform(jax.random.fold_in(own, dim), (parts,), jnp.float32, least / len(cuts), top_value / len(cuts)))
        gain = gain * jnp.repeat(draws, shape[dim] // parts).reshape([-1 if axis == dim else 1 for axis in range(len(shape))])
    return gain


def normal_values(key, extent, scale, most, cuts=(), kind=jnp.bfloat16):
    values = scale * jax.random.normal(key, extent, jnp.float32)
    if cuts:
        values = values * levels(key, extent, cuts, -0.22, 0.18)
    return jnp.clip(values, -most, most).astype(kind)


def setup_inputs(seed: int = 0, part: int = 0) -> dict:
    streams_of = jax.random.split(jax.random.key(seed), 9)
    part_splits = jax.random.split(jax.random.fold_in(streams_of[8], part), 9)
    return {
        "wind_east": normal_values(part_splits[0], (LEVELS, NLAT, NLON), 1.0, 6.0, ((0, 2), (1, 4), (2, 2)), jnp.float32),
        "wind_north": normal_values(part_splits[1], (LEVELS, NLAT, NLON), 1.0, 6.0, ((0, 2), (1, 4), (2, 2)), jnp.float32),
        "thickness": normal_values(part_splits[2], (LEVELS, NLAT, NLON), 1.0, 6.0, ((0, 2), (1, 4), (2, 2)), jnp.float32),
        "geopot": normal_values(part_splits[3], (LEVELS, NLAT, NLON), 1.0, 6.0, ((0, 2), (1, 4), (2, 2)), jnp.float32),
        "surface_geopot": normal_values(streams_of[4], (NLAT, NLON), 1.0, 6.0, ((0, 4), (1, 2)), jnp.float32),
        "mean_depth": jnp.clip(jnp.exp(math.log(2.0) - 1.3862944 * jax.random.uniform(streams_of[5], (LEVELS,), jnp.float32) ** levels(streams_of[5], (LEVELS,), ((0, 2),), -0.2, 0.2)), 0.5, 2.0),
        "kept_modes": draw_kept_modes(jax.random.fold_in(streams_of[8], 71), part),
        "slot_table": draw_slot_table(jax.random.fold_in(streams_of[8], 71), part),
    }


STEP_FACTOR = 0.15
CORIOLIS = 0.2
GRAVITY = 0.25


def east_diff(stacked):
    return jnp.roll(stacked, -1, axis=-1) - jnp.roll(stacked, 1, axis=-1)


def north_diff(stacked):
    padded = jnp.pad(stacked, ((0, 0), (1, 1), (0, 0)))
    return padded[:, 2:, :] - padded[:, :-2, :]


def reference(wind_east, wind_north, thickness, geopot, surface_geopot, mean_depth, kept_modes, slot_table):
    lam_step = 2.0 * math.pi / NLON
    phi_step = math.pi / NLAT
    latitude = -0.5 * math.pi + (jnp.arange(NLAT, dtype=jnp.float32) + 0.5) * phi_step
    coslat = jnp.cos(latitude)[:, None]
    sinlat = jnp.sin(latitude)[:, None]
    east_coef = STEP_FACTOR / coslat
    north_coef = STEP_FACTOR * lam_step / phi_step
    east_new = wind_east - east_coef * east_diff(geopot) + CORIOLIS * sinlat * wind_north
    north_new = wind_north - north_coef * north_diff(geopot) - CORIOLIS * sinlat * wind_east
    polar_rows = jnp.concatenate([jnp.arange(NP), jnp.arange(NLAT - NP, NLAT)]).astype(jnp.int32)
    wind_pair = jnp.stack([east_new, north_new])
    polar_part = wind_pair[:, :, polar_rows, :]
    transform = jnp.fft.rfft(polar_part, axis=-1)[..., :KMAX]
    wavenumber = jnp.arange(KMAX)
    weight = jnp.where(wavenumber == 0, 1.0, 2.0) / NLON
    keep_mask = wavenumber[None, :] < kept_modes[:, None]
    factor = jnp.where(keep_mask, weight[None, :], 0.0)
    cos_part = jnp.real(transform) * factor
    sin_part = -jnp.imag(transform) * factor
    ordered = jnp.concatenate([cos_part, sin_part], axis=-1)
    spectra = jnp.zeros_like(ordered).at[:, :, slot_table, :].set(ordered)
    masked = jnp.where(keep_mask, transform, jnp.zeros_like(transform))
    masked = jnp.pad(masked, ((0, 0), (0, 0), (0, 0), (0, NLON // 2 + 1 - KMAX)))
    filtered = jnp.fft.irfft(masked, n=NLON, axis=-1)
    wind_pair = wind_pair.at[:, :, polar_rows, :].set(filtered)
    east_final = wind_pair[0]
    north_final = wind_pair[1]
    divergence = east_coef * east_diff(east_final) + (north_coef / coslat) * north_diff(north_final * coslat)
    thick_new = thickness - mean_depth[:, None, None] * divergence
    column = jnp.cumsum(thick_new[::-1], axis=0)[::-1]
    geo_new = surface_geopot[None] + GRAVITY * column
    return (east_final, north_final, thick_new, geo_new, spectra)
```

```python
import math

import jax
import numpy as np
import jax.numpy as jnp
from jax import lax
from jax.sharding import PartitionSpec as P

KMAX = 360


STEP_FACTOR = 0.15
CORIOLIS = 0.2
GRAVITY = 0.25


def edges(block, axis, dim, periodic):
    count = lax.axis_size(axis)
    first = lax.slice_in_dim(block, 0, 1, axis=dim)
    last = lax.slice_in_dim(block, block.shape[dim] - 1, block.shape[dim], axis=dim)
    if periodic and count == 2:
        both = lax.ppermute(jnp.concatenate([last, first], axis=dim), axis, [(0, 1), (1, 0)])
        return lax.slice_in_dim(both, 0, 1, axis=dim), lax.slice_in_dim(both, 1, 2, axis=dim)
    forward = [(i, i + 1) for i in range(count - 1)]
    if periodic:
        forward.append((count - 1, 0))
    backward = [(target, source) for source, target in forward]
    return lax.ppermute(last, axis, forward), lax.ppermute(first, axis, backward)


def diff(block, low, high, dim):
    size = block.shape[dim]
    up = jnp.concatenate([lax.slice_in_dim(block, 1, size, axis=dim), high], axis=dim)
    down = jnp.concatenate([low, lax.slice_in_dim(block, 0, size - 1, axis=dim)], axis=dim)
    return up - down


def local_basis(count, nlon_total):
    fine = next(f for f in (24, 20, 18, 16, 12, 8, 6, 5, 4, 3, 2, 1) if count % f == 0)
    k = np.arange(KMAX, dtype=np.int64)[None, :]
    angle = 2.0 * np.pi / nlon_total

    def table(columns):
        phase = (columns[:, None] * k % nlon_total) * angle
        return np.cos(phase).astype(np.float32), np.sin(phase).astype(np.float32)

    cc, cs = (jnp.asarray(t)[:, None] for t in table(np.arange(0, count, fine)))
    fc, fs = (jnp.asarray(t)[None] for t in table(np.arange(fine)))
    return (
        (cc * fc - cs * fs).reshape(count, KMAX),
        (cs * fc + cc * fs).reshape(count, KMAX),
    )


def turned(pair, cos_shift, sin_shift):
    cos_part, sin_part = pair[..., :KMAX], pair[..., KMAX:]
    return jnp.concatenate(
        [cos_shift * cos_part - sin_shift * sin_part, sin_shift * cos_part + cos_shift * sin_part],
        axis=-1,
    )


def local(
    wind_east, wind_north, thickness, geopot, surface_geopot, mean_depth, kept_modes, slot_table
):
    lev_dev, lat_dev, lon_dev = thickness.shape
    lat_count = lax.axis_size("lat")
    lon_count = lax.axis_size("lon")
    lev_count = lax.axis_size("lev")
    lat_index = lax.axis_index("lat")
    lon_index = lax.axis_index("lon")
    nlat_total = lat_dev * lat_count
    nlon_total = lon_dev * lon_count
    polar_count = nlat_total // 4
    slot_count = 2 * polar_count
    help_rows = lat_dev // 2
    half_axis = lat_count // 2
    lam_step = 2.0 * math.pi / nlon_total
    phi_step = math.pi / nlat_total
    global_rows = lat_index * lat_dev + jnp.arange(lat_dev, dtype=jnp.int32)
    latitude = -0.5 * math.pi + (global_rows.astype(jnp.float32) + 0.5) * phi_step
    coslat = jnp.cos(latitude)[:, None]
    sinlat = jnp.sin(latitude)[:, None]
    east_coef = STEP_FACTOR / coslat
    north_coef = STEP_FACTOR * lam_step / phi_step
    geo_west, geo_east = edges(geopot, "lon", 2, True)
    geo_south, geo_north = edges(geopot, "lat", 1, False)
    east_new = (
        wind_east
        - east_coef * diff(geopot, geo_west, geo_east, 2)
        + CORIOLIS * sinlat * wind_north
    )
    north_new = (
        wind_north
        - north_coef * diff(geopot, geo_south, geo_north, 1)
        - CORIOLIS * sinlat * wind_east
    )
    is_polar = (lat_index < lat_count // 4) | (lat_index >= lat_count - lat_count // 4)
    first_row = lat_index * lat_dev
    first_rank = jnp.where(lat_index < lat_count // 4, first_row, first_row - (nlat_total - slot_count))
    first_rank = jnp.clip(first_rank, 0, slot_count - lat_dev)
    kept = lax.dynamic_slice(kept_modes, (first_rank,), (lat_dev,))
    slots = lax.dynamic_slice(slot_table, (first_rank,), (lat_dev,))
    wavenumber = jnp.arange(2 * KMAX, dtype=jnp.int32) % KMAX
    weight = (jnp.where(wavenumber == 0, 1.0, 2.0) / nlon_total).astype(jnp.float32)
    factor = jnp.where(wavenumber[None, :] < kept[:, None], weight[None, :], 0.0)
    cos_basis, sin_basis = local_basis(lon_dev, nlon_total)
    basis = jnp.concatenate([cos_basis, sin_basis], axis=1)
    shift = (lon_index * jnp.arange(KMAX, dtype=jnp.int32) % lon_count).astype(jnp.float32)
    shift = shift * (2.0 * math.pi / lon_count)
    if lon_count == 2:
        cos_shift = 1.0 - 2.0 * (lon_index * jnp.arange(KMAX, dtype=jnp.int32) % 2).astype(jnp.float32)
        sin_shift = jnp.zeros_like(cos_shift)
    else:
        cos_shift, sin_shift = jnp.cos(shift), jnp.sin(shift)
    pieces = [wind[level] for level in range(lev_dev) for wind in (east_new, north_new)]
    both_sums = []
    for piece in range(lev_dev):
        rows = jnp.concatenate(pieces[2 * piece : 2 * piece + 2], axis=0)
        part = jnp.dot(rows, basis, precision=lax.Precision.HIGH)
        part = turned(part, cos_shift, sin_shift)
        if lon_count == 2:
            sums = part + lax.ppermute(part, "lon", [(0, 1), (1, 0)])
        else:
            sums = lax.psum(part, "lon")
        both_sums.append(sums.reshape(2, lat_dev, 2 * KMAX) * factor[None])
    filtered = []
    for sums in both_sums:
        turned_back = turned(sums, cos_shift, -sin_shift)
        rows = lax.dot_general(
            turned_back.reshape(2 * lat_dev, 2 * KMAX),
            basis,
            (((1,), (1,)), ((), ())),
            precision=lax.Precision.HIGH,
        )
        filtered.append(rows.reshape(2, lat_dev, lon_dev))
    filtered = jnp.stack(filtered, axis=1)
    east_final = jnp.where(is_polar, filtered[0], east_new)
    north_final = jnp.where(is_polar, filtered[1], north_new)

    slice_width = 2 * KMAX // lon_count
    kept_sums = jnp.stack(both_sums, axis=1)
    own = lax.dynamic_slice_in_dim(kept_sums, lon_index * slice_width, slice_width, 3)
    places = jnp.arange(help_rows, dtype=jnp.int32)
    partner = (lat_index + half_axis) % lat_count

    def rows_named(device):
        match = slots[None, :] == (device * help_rows + places)[:, None]
        return jnp.einsum(
            "sr,abrc->absc", match.astype(jnp.float32), own, precision=lax.Precision.HIGHEST
        )

    route = [((i - half_axis) % lat_count, i) for i in range(lat_count)]
    route = [(s, t) for s, t in route if s < lat_count // 4 or s >= lat_count - lat_count // 4]
    arrived = lax.ppermute(rows_named(partner), "lat", route)
    spectra = jnp.where(is_polar, rows_named(lat_index), arrived)

    rim_west, rim_east = edges(east_final, "lon", 2, True)
    flux = north_final * coslat
    rim_south, rim_north = edges(flux, "lat", 1, False)
    divergence = east_coef * diff(east_final, rim_west, rim_east, 2) + north_coef / coslat * diff(
        flux, rim_south, rim_north, 1
    )
    thick_new = thickness - mean_depth[:, None, None] * divergence
    columns = [thick_new[lev_dev - 1]]
    for level in range(lev_dev - 2, -1, -1):
        columns.append(columns[-1] + thick_new[level])
    columns = columns[::-1]
    deeper = jnp.zeros_like(columns[0])
    for distance in range(1, lev_count):
        deeper = deeper + lax.ppermute(
            columns[0], "lev", [(i + distance, i) for i in range(lev_count - distance)]
        )
    geo_new = surface_geopot[None] + GRAVITY * (jnp.stack(columns) + deeper[None])
    return (east_final, north_final, thick_new, geo_new, spectra)


def solution(mesh):
    return jax.shard_map(
        local,
        mesh=mesh,
        in_specs=(
            P(("members", "lev"), "lat", "lon"),
            P(("members", "lev"), "lat", "lon"),
            P(("members", "lev"), "lat", "lon"),
            P(("members", "lev"), "lat", "lon"),
            P("lat", "lon"),
            P("lev"),
            P(),
            P(),
        ),
        out_specs=(
            P(("members", "lev"), "lat", "lon"),
            P(("members", "lev"), "lat", "lon"),
            P(("members", "lev"), "lat", "lon"),
            P(("members", "lev"), "lat", "lon"),
            P(None, ("members", "lev"), "lat", "lon"),
        ),
        check_vma=False,
    )
```

```python
import math

import functools

import jax
import numpy as np
import jax.numpy as jnp
from jax import lax
from jax.experimental import pallas as pl
from jax.experimental.pallas import tpu as pltpu
from jax.sharding import PartitionSpec as P

KMAX = 360


STEP_FACTOR = 0.15
CORIOLIS = 0.2
GRAVITY = 0.25


def edges(block, axis, dim, periodic):
    count = lax.axis_size(axis)
    first = lax.slice_in_dim(block, 0, 1, axis=dim)
    last = lax.slice_in_dim(block, block.shape[dim] - 1, block.shape[dim], axis=dim)
    if periodic and count == 2:
        both = lax.ppermute(jnp.concatenate([last, first], axis=dim), axis, [(0, 1), (1, 0)])
        return lax.slice_in_dim(both, 0, 1, axis=dim), lax.slice_in_dim(both, 1, 2, axis=dim)
    forward = [(i, i + 1) for i in range(count - 1)]
    if periodic:
        forward.append((count - 1, 0))
    backward = [(target, source) for source, target in forward]
    return lax.ppermute(last, axis, forward), lax.ppermute(first, axis, backward)


def diff(block, low, high, dim):
    size = block.shape[dim]
    up = jnp.concatenate([lax.slice_in_dim(block, 1, size, axis=dim), high], axis=dim)
    down = jnp.concatenate([low, lax.slice_in_dim(block, 0, size - 1, axis=dim)], axis=dim)
    return up - down


def local_basis(count, nlon_total):
    fine = next(f for f in (24, 20, 18, 16, 12, 8, 6, 5, 4, 3, 2, 1) if count % f == 0)
    k = np.arange(KMAX, dtype=np.int64)[None, :]
    angle = 2.0 * np.pi / nlon_total

    def table(columns):
        phase = (columns[:, None] * k % nlon_total) * angle
        return np.cos(phase).astype(np.float32), np.sin(phase).astype(np.float32)

    cc, cs = (jnp.asarray(t)[:, None] for t in table(np.arange(0, count, fine)))
    fc, fs = (jnp.asarray(t)[None] for t in table(np.arange(fine)))
    return (
        (cc * fc - cs * fs).reshape(count, KMAX),
        (cs * fc + cc * fs).reshape(count, KMAX),
    )


def turned(pair, cos_shift, sin_shift):
    cos_part, sin_part = pair[..., :KMAX], pair[..., KMAX:]
    return jnp.concatenate(
        [cos_shift * cos_part - sin_shift * sin_part, sin_shift * cos_part + cos_shift * sin_part],
        axis=-1,
    )


def local(
    wind_east, wind_north, thickness, geopot, surface_geopot, mean_depth, kept_modes, slot_table
):
    lev_dev, lat_dev, lon_dev = thickness.shape
    lat_count = lax.axis_size("lat")
    lon_count = lax.axis_size("lon")
    lev_count = lax.axis_size("lev")
    lat_index = lax.axis_index("lat")
    lon_index = lax.axis_index("lon")
    nlat_total = lat_dev * lat_count
    nlon_total = lon_dev * lon_count
    polar_count = nlat_total // 4
    slot_count = 2 * polar_count
    help_rows = lat_dev // 2
    half_axis = lat_count // 2
    lam_step = 2.0 * math.pi / nlon_total
    phi_step = math.pi / nlat_total
    global_rows = lat_index * lat_dev + jnp.arange(lat_dev, dtype=jnp.int32)
    latitude = -0.5 * math.pi + (global_rows.astype(jnp.float32) + 0.5) * phi_step
    coslat = jnp.cos(latitude)[:, None]
    sinlat = jnp.sin(latitude)[:, None]
    east_coef = STEP_FACTOR / coslat
    north_coef = STEP_FACTOR * lam_step / phi_step
    geo_west, geo_east = edges(geopot, "lon", 2, True)
    geo_south, geo_north = edges(geopot, "lat", 1, False)
    east_new = (
        wind_east
        - east_coef * diff(geopot, geo_west, geo_east, 2)
        + CORIOLIS * sinlat * wind_north
    )
    north_new = (
        wind_north
        - north_coef * diff(geopot, geo_south, geo_north, 1)
        - CORIOLIS * sinlat * wind_east
    )
    is_polar = (lat_index < lat_count // 4) | (lat_index >= lat_count - lat_count // 4)
    first_row = lat_index * lat_dev
    first_rank = jnp.where(lat_index < lat_count // 4, first_row, first_row - (nlat_total - slot_count))
    first_rank = jnp.clip(first_rank, 0, slot_count - lat_dev)
    kept = lax.dynamic_slice(kept_modes, (first_rank,), (lat_dev,))
    slots = lax.dynamic_slice(slot_table, (first_rank,), (lat_dev,))
    wavenumber = jnp.arange(2 * KMAX, dtype=jnp.int32) % KMAX
    weight = (jnp.where(wavenumber == 0, 1.0, 2.0) / nlon_total).astype(jnp.float32)
    factor = jnp.where(wavenumber[None, :] < kept[:, None], weight[None, :], 0.0)
    cos_basis, sin_basis = local_basis(lon_dev, nlon_total)
    basis = jnp.concatenate([cos_basis, sin_basis], axis=1)
    shift = (lon_index * jnp.arange(KMAX, dtype=jnp.int32) % lon_count).astype(jnp.float32)
    shift = shift * (2.0 * math.pi / lon_count)
    if lon_count == 2:
        cos_shift = 1.0 - 2.0 * (lon_index * jnp.arange(KMAX, dtype=jnp.int32) % 2).astype(jnp.float32)
        sin_shift = jnp.zeros_like(cos_shift)
    else:
        cos_shift, sin_shift = jnp.cos(shift), jnp.sin(shift)
    pieces = [wind[level] for level in range(lev_dev) for wind in (east_new, north_new)]
    both_sums = []
    for piece in range(lev_dev):
        rows = jnp.concatenate(pieces[2 * piece : 2 * piece + 2], axis=0)
        part = jnp.dot(rows, basis, precision=lax.Precision.HIGH)
        part = turned(part, cos_shift, sin_shift)
        if lon_count == 2:
            sums = part + lax.ppermute(part, "lon", [(0, 1), (1, 0)])
        else:
            sums = lax.psum(part, "lon")
        both_sums.append(sums.reshape(2, lat_dev, 2 * KMAX) * factor[None])
    filtered = []
    for sums in both_sums:
        turned_back = turned(sums, cos_shift, -sin_shift)
        rows = lax.dot_general(
            turned_back.reshape(2 * lat_dev, 2 * KMAX),
            basis,
            (((1,), (1,)), ((), ())),
            precision=lax.Precision.HIGH,
        )
        filtered.append(rows.reshape(2, lat_dev, lon_dev))
    filtered = jnp.stack(filtered, axis=1)
    east_final = jnp.where(is_polar, filtered[0], east_new)
    north_final = jnp.where(is_polar, filtered[1], north_new)

    slice_width = 2 * KMAX // lon_count
    kept_sums = jnp.stack(both_sums, axis=1)
    own = lax.dynamic_slice_in_dim(kept_sums, lon_index * slice_width, slice_width, 3)
    places = jnp.arange(help_rows, dtype=jnp.int32)
    partner = (lat_index + half_axis) % lat_count

    def rows_named(device):
        match = slots[None, :] == (device * help_rows + places)[:, None]
        return jnp.einsum(
            "sr,abrc->absc", match.astype(jnp.float32), own, precision=lax.Precision.HIGHEST
        )

    route = [((i - half_axis) % lat_count, i) for i in range(lat_count)]
    route = [(s, t) for s, t in route if s < lat_count // 4 or s >= lat_count - lat_count // 4]
    arrived = lax.ppermute(rows_named(partner), "lat", route)
    spectra = jnp.where(is_polar, rows_named(lat_index), arrived)

    rim_west, rim_east = edges(east_final, "lon", 2, True)
    flux = north_final * coslat
    rim_south, rim_north = edges(flux, "lat", 1, False)
    divergence = east_coef * diff(east_final, rim_west, rim_east, 2) + north_coef / coslat * diff(
        flux, rim_south, rim_north, 1
    )
    thick_new = thickness - mean_depth[:, None, None] * divergence
    columns = [thick_new[lev_dev - 1]]
    for level in range(lev_dev - 2, -1, -1):
        columns.append(columns[-1] + thick_new[level])
    columns = columns[::-1]
    deeper = jnp.zeros_like(columns[0])
    for distance in range(1, lev_count):
        deeper = deeper + lax.ppermute(
            columns[0], "lev", [(i + distance, i) for i in range(lev_count - distance)]
        )
    geo_new = surface_geopot[None] + GRAVITY * (jnp.stack(columns) + deeper[None])
    return (east_final, north_final, thick_new, geo_new, spectra)


FINE = 32


def angle_tables(count, nlon_total):
    k = np.arange(KMAX, dtype=np.int64)[None, :]
    angle = 2.0 * np.pi / nlon_total

    def table(columns):
        phase = (columns[:, None] * k % nlon_total) * angle
        return np.cos(phase), np.sin(phase)

    cc, cs = table(np.arange(0, count, FINE))
    fc, fs = table(np.arange(FINE))
    coarse = np.stack([np.concatenate([cc, cs], 1), np.concatenate([-cs, cc], 1)])
    fine = np.stack([np.concatenate([fc, fc], 1), np.concatenate([fs, fs], 1)])
    return coarse.astype(np.float32), fine.astype(np.float32)


def split(x):
    high = x.astype(jnp.bfloat16)
    return high, (x - high.astype(jnp.float32)).astype(jnp.bfloat16)


def three_pass(x, high_ref, low_ref, dims):
    high, low = split(x)
    rows = x.shape[0]

    def dot(a, b):
        return lax.dot_general(a, b, (dims, ((), ())), preferred_element_type=jnp.float32)

    basis = high_ref[...]
    return dot(high, basis) + dot(low, basis) + dot(high, low_ref[...])


def substep_kernel(
    sizes,
    depth_ref, kept_ref, slot_ref, row_ref, coarse_ref, fine_ref,
    we_hbm, wn_hbm, th_hbm, geo_hbm, sg_hbm,
    east_out, north_out, thick_out, geo_out, spectra_out,
    we, wn, th, geo, sg, rows_ref, high_ref, low_ref, part, came,
    lon_put, lon_got, lat_put, lat_got, column_put, column_got, spec_put, spec_got,
    in_sem, lon_sem, lat_sem, part_sem, column_sem, spec_sem,
):
    lat_count, polar_bands, half_axis, nlon_total, north_coef = sizes
    lev_dev, lat_dev, lon_dev = we.shape
    help_rows = spec_put.shape[1]
    lon = lax.axis_index("lon")
    lat = lax.axis_index("lat")
    lev = lax.axis_index("lev")
    other_lon = {"lon": 1 - lon}
    other_lev = {"lev": 1 - lev}
    partner = lax.rem(lat + half_axis, lat_count)
    far = {"lat": partner}
    has_south = lat > 0
    has_north = lat < lat_count - 1
    polar = (lat < polar_bands) | (lat >= lat_count - polar_bands)
    MESH = pl.DeviceIdType.MESH

    loads = [
        pltpu.make_async_copy(src, dst, in_sem.at[i])
        for i, (src, dst) in enumerate(
            ((geo_hbm, geo), (we_hbm, we), (wn_hbm, wn), (th_hbm, th), (sg_hbm, sg))
        )
    ]
    for load in loads:
        load.start()

    barrier = pltpu.get_barrier_semaphore()
    for target in (other_lon, other_lev, far):
        pl.semaphore_signal(barrier, inc=1, device_id=target, device_id_type=MESH)

    @pl.when(has_south)
    def _():
        pl.semaphore_signal(barrier, inc=1, device_id={"lat": lat - 1}, device_id_type=MESH)

    @pl.when(has_north)
    def _():
        pl.semaphore_signal(barrier, inc=1, device_id={"lat": lat + 1}, device_id_type=MESH)

    pl.semaphore_wait(barrier, 3 + has_south.astype(jnp.int32) + has_north.astype(jnp.int32))

    def remote(src, dst, sems, target):
        return pltpu.make_async_remote_copy(
            src_ref=src, dst_ref=dst, send_sem=sems.at[0], recv_sem=sems.at[1],
            device_id=target, device_id_type=MESH,
        )

    lane = lax.broadcasted_iota(jnp.int32, (lat_dev, lon_dev), 1)
    row = lax.broadcasted_iota(jnp.int32, (lat_dev, lon_dev), 0)
    edge_lane = lax.broadcasted_iota(jnp.int32, (lat_dev, 128), 1)

    def send_lon(turn, field):
        held = jnp.zeros((lat_dev, 128), jnp.float32)
        for level in range(lev_dev):
            held = jnp.where(edge_lane == 2 * level, field[level, :, 0:1], held)
            held = jnp.where(edge_lane == 2 * level + 1, field[level, :, lon_dev - 1 : lon_dev], held)
        lon_put[turn, :, 0:lat_dev] = jnp.transpose(held)[0:8]
        copy = remote(lon_put.at[turn], lon_got.at[turn], lon_sem.at[turn], other_lon)
        copy.start()
        return copy

    def send_lat(turn, field, scale):
        for level in range(lev_dev):
            lat_put[turn, 0, level : level + 1, :] = field[level, 0:1, :] * scale[0:1]
            lat_put[turn, 1, level : level + 1, :] = (
                field[level, lat_dev - 1 : lat_dev, :] * scale[lat_dev - 1 : lat_dev]
            )
        south = remote(lat_put.at[turn, 0], lat_got.at[turn, 1], lat_sem.at[turn, 0], {"lat": lat - 1})
        north = remote(lat_put.at[turn, 1], lat_got.at[turn, 0], lat_sem.at[turn, 1], {"lat": lat + 1})

        @pl.when(has_south)
        def _():
            south.start()

        @pl.when(has_north)
        def _():
            north.start()

        @pl.when(jnp.logical_not(has_south))
        def _():
            lat_got[turn, 0] = jnp.zeros_like(lat_got[turn, 0])

        @pl.when(jnp.logical_not(has_north))
        def _():
            lat_got[turn, 1] = jnp.zeros_like(lat_got[turn, 1])

        return south, north

    def wait_lat(south, north):
        @pl.when(has_south)
        def _():
            south.wait_send()
            north.wait_recv()

        @pl.when(has_north)
        def _():
            north.wait_send()
            south.wait_recv()

    def east_diff(x, turn, level, rims):
        first = rims[:, 2 * level : 2 * level + 1]
        last = rims[:, 2 * level + 1 : 2 * level + 2]
        up = jnp.where(lane == lon_dev - 1, first, pltpu.roll(x, lon_dev - 1, 1))
        down = jnp.where(lane == 0, last, pltpu.roll(x, 1, 1))
        return up - down

    def north_diff(x, turn, level):
        up = jnp.concatenate([x[1:], lat_got[turn, 1, level : level + 1, :]], axis=0)
        down = jnp.concatenate([lat_got[turn, 0, level : level + 1, :], x[:-1]], axis=0)
        return up - down

    cos_lat = row_ref[:, 0:1]
    sin_lat = row_ref[:, 1:2]
    east_coef = row_ref[:, 2:3]
    flux_coef = row_ref[:, 3:4]
    one = jnp.ones((lat_dev, 1), jnp.float32)

    loads[0].wait()
    lon_copy = send_lon(0, geo)
    lat_copies = send_lat(0, geo, one)

    def make_basis(block, _):
        p = coarse_ref[0, pl.ds(block, 1), :]
        q = coarse_ref[1, pl.ds(block, 1), :]
        values = p * fine_ref[0] + q * fine_ref[1]
        high, low = split(values)
        at = pl.ds(pl.multiple_of(block * FINE, FINE), FINE)
        high_ref[at, :] = high
        low_ref[at, :] = low
        return _

    lax.fori_loop(0, lon_dev // FINE, make_basis, 0)
    for load in loads[1:]:
        load.wait()
    lon_copy.wait()
    wait_lat(*lat_copies)

    rims = jnp.transpose(lon_got[0])[0:lat_dev]
    part_copies = []
    for level in range(lev_dev):
        x = geo[level]
        east = we[level]
        north = wn[level]
        east_new = east - east_coef * east_diff(x, 0, level, rims) + CORIOLIS * sin_lat * north
        north_new = north - north_coef * north_diff(x, 0, level) - CORIOLIS * sin_lat * east
        rows_ref[level, 0:lat_dev, :] = east_new
        rows_ref[level, lat_dev:, :] = north_new
        east_out[level] = east_new
        north_out[level] = north_new
        part[level] = three_pass(rows_ref[level], high_ref, low_ref, ((1,), (0,)))
        copy = remote(part.at[level], came.at[level], part_sem.at[level], other_lon)
        copy.start()
        part_copies.append(copy)

    column_id = lax.broadcasted_iota(jnp.int32, (lat_dev, 2 * KMAX), 1)
    wavenumber = jnp.where(column_id < KMAX, column_id, column_id - KMAX)
    weight = jnp.where(wavenumber == 0, 1.0 / nlon_total, 2.0 / nlon_total)
    odd = 1.0 - 2.0 * lax.rem(wavenumber, 2).astype(jnp.float32)
    first = jnp.where(lat < polar_bands, lat, jnp.maximum(lat - (lat_count - 2 * polar_bands), 0))
    first = jnp.minimum(first, 2 * polar_bands - 1)
    kept = kept_ref[first]
    slots = slot_ref[first]
    factor = jnp.where(wavenumber < kept, weight, 0.0)
    factor2 = jnp.concatenate([factor, factor], axis=0)
    odd_row = odd[0:1]
    for level in range(lev_dev):
        part_copies[level].wait()
        kept_sums = (part[level] + odd_row * came[level]) * factor2
        came[level] = kept_sums
        filtered = three_pass(kept_sums, high_ref, low_ref, ((1,), (1,)))

        @pl.when(polar)
        def _():
            east_out[level] = filtered[0:lat_dev]
            north_out[level] = filtered[lat_dev:]

    lon_copy = send_lon(1, east_out)
    lat_copies = send_lat(1, north_out, cos_lat)

    place = lax.broadcasted_iota(jnp.int32, (lat_dev, help_rows), 1)
    match_own = (slots == lat * help_rows + place).astype(jnp.float32)
    match_far = (slots == partner * help_rows + place).astype(jnp.float32)

    def gathered(match, level, wind):
        values = came[level, wind * lat_dev : (wind + 1) * lat_dev, :]
        picked = lax.dot_general(
            match, values, (((0,), (0,)), ((), ())),
            precision=lax.Precision.HIGHEST, preferred_element_type=jnp.float32,
        )
        spun = picked * odd[0:help_rows]
        return jnp.where(lon == 0, picked[:, 0:KMAX], spun[:, KMAX:])

    spec_copy = remote(spec_put, spec_got, spec_sem, far)

    @pl.when(polar)
    def _():
        for wind in range(2):
            for level in range(lev_dev):
                spec_put[wind * lev_dev + level] = gathered(match_far, level, wind)
        spec_copy.start()
        for wind in range(2):
            for level in range(lev_dev):
                spectra_out[wind, level] = gathered(match_own, level, wind)

    lon_copy.wait()
    wait_lat(*lat_copies)
    rims = jnp.transpose(lon_got[1])[0:lat_dev]
    below = None
    for level in range(lev_dev - 1, -1, -1):
        flux = north_out[level] * cos_lat
        divergence = east_coef * east_diff(east_out[level], 1, level, rims) + flux_coef * north_diff(
            flux, 1, level
        )
        thick = th[level] - depth_ref[level] * divergence
        thick_out[level] = thick
        below = thick if below is None else below + thick
        geo_out[level] = below
    column_put[...] = below
    column_copy = remote(column_put, column_got, column_sem, other_lev)

    @pl.when(lev == 1)
    def _():
        column_copy.start()
        for level in range(lev_dev):
            geo_out[level] = sg[...] + GRAVITY * geo_out[level]

    @pl.when(lev == 0)
    def _():
        column_copy.wait_recv()
        for level in range(lev_dev):
            geo_out[level] = sg[...] + GRAVITY * (geo_out[level] + column_got[...])

    @pl.when(lev == 1)
    def _():
        column_copy.wait_send()

    @pl.when(polar)
    def _():
        spec_copy.wait_send()

    @pl.when(jnp.logical_not(polar))
    def _():
        spec_copy.wait_recv()
        for wind in range(2):
            for level in range(lev_dev):
                spectra_out[wind, level] = spec_got[wind * lev_dev + level]


def one_kernel(
    wind_east, wind_north, thickness, geopot, surface_geopot, mean_depth, kept_modes, slot_table
):
    lev_dev, lat_dev, lon_dev = thickness.shape
    lat_count = lax.axis_size("lat")
    nlat_total = lat_dev * lat_count
    nlon_total = 2 * lon_dev
    help_rows = lat_dev // 2
    lam_step = 2.0 * math.pi / nlon_total
    phi_step = math.pi / nlat_total
    north_coef = STEP_FACTOR * lam_step / phi_step
    global_rows = lax.axis_index("lat") * lat_dev + jnp.arange(lat_dev, dtype=jnp.int32)
    latitude = -0.5 * math.pi + (global_rows.astype(jnp.float32) + 0.5) * phi_step
    coslat = jnp.cos(latitude)
    row_table = jnp.stack(
        [coslat, jnp.sin(latitude), STEP_FACTOR / coslat, north_coef / coslat], axis=1
    )
    bands = 2 * (lat_count // 4)
    coarse, fine = angle_tables(lon_dev, nlon_total)
    whole = pl.BlockSpec(memory_space=pltpu.VMEM)
    away = pl.BlockSpec(memory_space=pl.ANY)
    field = jax.ShapeDtypeStruct((lev_dev, lat_dev, lon_dev), jnp.float32)
    block = pltpu.VMEM((lev_dev, lat_dev, lon_dev), jnp.float32)
    basis = pltpu.VMEM((lon_dev, 2 * KMAX), jnp.bfloat16)
    sums = pltpu.VMEM((lev_dev, 2 * lat_dev, 2 * KMAX), jnp.float32)
    specs = pltpu.VMEM((2 * lev_dev, help_rows, KMAX), jnp.float32)
    dma = pltpu.SemaphoreType.DMA
    return pl.pallas_call(
        functools.partial(
            substep_kernel,
            (lat_count, lat_count // 4, lat_count // 2, nlon_total, north_coef),
        ),
        out_shape=(field,) * 4
        + (jax.ShapeDtypeStruct((2, lev_dev, help_rows, KMAX), jnp.float32),),
        in_specs=[pl.BlockSpec(memory_space=pltpu.SMEM)] + [whole] * 5 + [away] * 5,
        out_specs=(whole,) * 5,
        scratch_shapes=[
            block, block, block, block,
            pltpu.VMEM((lat_dev, lon_dev), jnp.float32),
            pltpu.VMEM((lev_dev, 2 * lat_dev, lon_dev), jnp.float32),
            basis, basis, sums, sums,
            pltpu.VMEM((2, 8, 128), jnp.float32),
            pltpu.VMEM((2, 8, 128), jnp.float32),
            pltpu.VMEM((2, 2, lev_dev, lon_dev), jnp.float32),
            pltpu.VMEM((2, 2, lev_dev, lon_dev), jnp.float32),
            pltpu.VMEM((lat_dev, lon_dev), jnp.float32),
            pltpu.VMEM((lat_dev, lon_dev), jnp.float32),
            specs, specs,
            dma((5,)), dma((2, 2)), dma((2, 2, 2)), dma((lev_dev, 2)), dma((2,)), dma((2,)),
        ],
        compiler_params=pltpu.CompilerParams(
            collective_id=0, has_side_effects=True, vmem_limit_bytes=60 * 2**20
        ),
    )(
        mean_depth,
        kept_modes.reshape(bands, lat_dev, 1),
        slot_table.reshape(bands, lat_dev, 1),
        row_table,
        jnp.asarray(coarse),
        jnp.asarray(fine),
        wind_east, wind_north, thickness, geopot, surface_geopot,
    )


def solution(mesh):
    body = one_kernel if mesh.shape["lon"] == 2 and mesh.shape["lev"] == 2 else local
    return jax.shard_map(
        body,
        mesh=mesh,
        in_specs=(
            P(("members", "lev"), "lat", "lon"),
            P(("members", "lev"), "lat", "lon"),
            P(("members", "lev"), "lat", "lon"),
            P(("members", "lev"), "lat", "lon"),
            P("lat", "lon"),
            P("lev"),
            P(),
            P(),
        ),
        out_specs=(
            P(("members", "lev"), "lat", "lon"),
            P(("members", "lev"), "lat", "lon"),
            P(("members", "lev"), "lat", "lon"),
            P(("members", "lev"), "lat", "lon"),
            P(None, ("members", "lev"), "lat", "lon"),
        ),
        check_vma=False,
    )
```

```python
import math

import functools

import jax
import numpy as np
import jax.numpy as jnp
from jax import lax
from jax.experimental import pallas as pl
from jax.experimental.pallas import tpu as pltpu
from jax.sharding import PartitionSpec as P

KMAX = 360


STEP_FACTOR = 0.15
CORIOLIS = 0.2
GRAVITY = 0.25


def edges(block, axis, dim, periodic):
    count = lax.axis_size(axis)
    first = lax.slice_in_dim(block, 0, 1, axis=dim)
    last = lax.slice_in_dim(block, block.shape[dim] - 1, block.shape[dim], axis=dim)
    if periodic and count == 2:
        both = lax.ppermute(jnp.concatenate([last, first], axis=dim), axis, [(0, 1), (1, 0)])
        return lax.slice_in_dim(both, 0, 1, axis=dim), lax.slice_in_dim(both, 1, 2, axis=dim)
    forward = [(i, i + 1) for i in range(count - 1)]
    if periodic:
        forward.append((count - 1, 0))
    backward = [(target, source) for source, target in forward]
    return lax.ppermute(last, axis, forward), lax.ppermute(first, axis, backward)


def diff(block, low, high, dim):
    size = block.shape[dim]
    up = jnp.concatenate([lax.slice_in_dim(block, 1, size, axis=dim), high], axis=dim)
    down = jnp.concatenate([low, lax.slice_in_dim(block, 0, size - 1, axis=dim)], axis=dim)
    return up - down


def local_basis(count, nlon_total):
    fine = next(f for f in (24, 20, 18, 16, 12, 8, 6, 5, 4, 3, 2, 1) if count % f == 0)
    k = np.arange(KMAX, dtype=np.int64)[None, :]
    angle = 2.0 * np.pi / nlon_total

    def table(columns):
        phase = (columns[:, None] * k % nlon_total) * angle
        return np.cos(phase).astype(np.float32), np.sin(phase).astype(np.float32)

    cc, cs = (jnp.asarray(t)[:, None] for t in table(np.arange(0, count, fine)))
    fc, fs = (jnp.asarray(t)[None] for t in table(np.arange(fine)))
    return (
        (cc * fc - cs * fs).reshape(count, KMAX),
        (cs * fc + cc * fs).reshape(count, KMAX),
    )


def turned(pair, cos_shift, sin_shift):
    cos_part, sin_part = pair[..., :KMAX], pair[..., KMAX:]
    return jnp.concatenate(
        [cos_shift * cos_part - sin_shift * sin_part, sin_shift * cos_part + cos_shift * sin_part],
        axis=-1,
    )


def local(
    wind_east, wind_north, thickness, geopot, surface_geopot, mean_depth, kept_modes, slot_table
):
    lev_dev, lat_dev, lon_dev = thickness.shape
    lat_count = lax.axis_size("lat")
    lon_count = lax.axis_size("lon")
    lev_count = lax.axis_size("lev")
    lat_index = lax.axis_index("lat")
    lon_index = lax.axis_index("lon")
    nlat_total = lat_dev * lat_count
    nlon_total = lon_dev * lon_count
    polar_count = nlat_total // 4
    slot_count = 2 * polar_count
    help_rows = lat_dev // 2
    half_axis = lat_count // 2
    lam_step = 2.0 * math.pi / nlon_total
    phi_step = math.pi / nlat_total
    global_rows = lat_index * lat_dev + jnp.arange(lat_dev, dtype=jnp.int32)
    latitude = -0.5 * math.pi + (global_rows.astype(jnp.float32) + 0.5) * phi_step
    coslat = jnp.cos(latitude)[:, None]
    sinlat = jnp.sin(latitude)[:, None]
    east_coef = STEP_FACTOR / coslat
    north_coef = STEP_FACTOR * lam_step / phi_step
    geo_west, geo_east = edges(geopot, "lon", 2, True)
    geo_south, geo_north = edges(geopot, "lat", 1, False)
    east_new = (
        wind_east
        - east_coef * diff(geopot, geo_west, geo_east, 2)
        + CORIOLIS * sinlat * wind_north
    )
    north_new = (
        wind_north
        - north_coef * diff(geopot, geo_south, geo_north, 1)
        - CORIOLIS * sinlat * wind_east
    )
    is_polar = (lat_index < lat_count // 4) | (lat_index >= lat_count - lat_count // 4)
    first_row = lat_index * lat_dev
    first_rank = jnp.where(lat_index < lat_count // 4, first_row, first_row - (nlat_total - slot_count))
    first_rank = jnp.clip(first_rank, 0, slot_count - lat_dev)
    kept = lax.dynamic_slice(kept_modes, (first_rank,), (lat_dev,))
    slots = lax.dynamic_slice(slot_table, (first_rank,), (lat_dev,))
    wavenumber = jnp.arange(2 * KMAX, dtype=jnp.int32) % KMAX
    weight = (jnp.where(wavenumber == 0, 1.0, 2.0) / nlon_total).astype(jnp.float32)
    factor = jnp.where(wavenumber[None, :] < kept[:, None], weight[None, :], 0.0)
    cos_basis, sin_basis = local_basis(lon_dev, nlon_total)
    basis = jnp.concatenate([cos_basis, sin_basis], axis=1)
    shift = (lon_index * jnp.arange(KMAX, dtype=jnp.int32) % lon_count).astype(jnp.float32)
    shift = shift * (2.0 * math.pi / lon_count)
    if lon_count == 2:
        cos_shift = 1.0 - 2.0 * (lon_index * jnp.arange(KMAX, dtype=jnp.int32) % 2).astype(jnp.float32)
        sin_shift = jnp.zeros_like(cos_shift)
    else:
        cos_shift, sin_shift = jnp.cos(shift), jnp.sin(shift)
    pieces = [wind[level] for level in range(lev_dev) for wind in (east_new, north_new)]
    both_sums = []
    for piece in range(lev_dev):
        rows = jnp.concatenate(pieces[2 * piece : 2 * piece + 2], axis=0)
        part = jnp.dot(rows, basis, precision=lax.Precision.HIGH)
        part = turned(part, cos_shift, sin_shift)
        if lon_count == 2:
            sums = part + lax.ppermute(part, "lon", [(0, 1), (1, 0)])
        else:
            sums = lax.psum(part, "lon")
        both_sums.append(sums.reshape(2, lat_dev, 2 * KMAX) * factor[None])
    filtered = []
    for sums in both_sums:
        turned_back = turned(sums, cos_shift, -sin_shift)
        rows = lax.dot_general(
            turned_back.reshape(2 * lat_dev, 2 * KMAX),
            basis,
            (((1,), (1,)), ((), ())),
            precision=lax.Precision.HIGH,
        )
        filtered.append(rows.reshape(2, lat_dev, lon_dev))
    filtered = jnp.stack(filtered, axis=1)
    east_final = jnp.where(is_polar, filtered[0], east_new)
    north_final = jnp.where(is_polar, filtered[1], north_new)

    slice_width = 2 * KMAX // lon_count
    kept_sums = jnp.stack(both_sums, axis=1)
    own = lax.dynamic_slice_in_dim(kept_sums, lon_index * slice_width, slice_width, 3)
    places = jnp.arange(help_rows, dtype=jnp.int32)
    partner = (lat_index + half_axis) % lat_count

    def rows_named(device):
        match = slots[None, :] == (device * help_rows + places)[:, None]
        return jnp.einsum(
            "sr,abrc->absc", match.astype(jnp.float32), own, precision=lax.Precision.HIGHEST
        )

    route = [((i - half_axis) % lat_count, i) for i in range(lat_count)]
    route = [(s, t) for s, t in route if s < lat_count // 4 or s >= lat_count - lat_count // 4]
    arrived = lax.ppermute(rows_named(partner), "lat", route)
    spectra = jnp.where(is_polar, rows_named(lat_index), arrived)

    rim_west, rim_east = edges(east_final, "lon", 2, True)
    flux = north_final * coslat
    rim_south, rim_north = edges(flux, "lat", 1, False)
    divergence = east_coef * diff(east_final, rim_west, rim_east, 2) + north_coef / coslat * diff(
        flux, rim_south, rim_north, 1
    )
    thick_new = thickness - mean_depth[:, None, None] * divergence
    columns = [thick_new[lev_dev - 1]]
    for level in range(lev_dev - 2, -1, -1):
        columns.append(columns[-1] + thick_new[level])
    columns = columns[::-1]
    deeper = jnp.zeros_like(columns[0])
    for distance in range(1, lev_count):
        deeper = deeper + lax.ppermute(
            columns[0], "lev", [(i + distance, i) for i in range(lev_count - distance)]
        )
    geo_new = surface_geopot[None] + GRAVITY * (jnp.stack(columns) + deeper[None])
    return (east_final, north_final, thick_new, geo_new, spectra)


FINE = 32


def angle_tables(count, nlon_total):
    k = np.arange(KMAX, dtype=np.int64)[None, :]
    angle = 2.0 * np.pi / nlon_total

    def table(columns):
        phase = (columns[:, None] * k % nlon_total) * angle
        return np.cos(phase), np.sin(phase)

    cc, cs = table(np.arange(0, count, FINE))
    fc, fs = table(np.arange(FINE))
    coarse = np.stack([np.concatenate([cc, cs], 1), np.concatenate([-cs, cc], 1)])
    fine = np.stack([np.concatenate([fc, fc], 1), np.concatenate([fs, fs], 1)])
    return coarse.astype(np.float32), fine.astype(np.float32)


def split(x):
    high = x.astype(jnp.bfloat16)
    return high, (x - high.astype(jnp.float32)).astype(jnp.bfloat16)


def three_pass(x, high_ref, low_ref, dims):
    high, low = split(x)
    rows = x.shape[0]

    def dot(a, b):
        return lax.dot_general(a, b, (dims, ((), ())), preferred_element_type=jnp.float32)

    basis = high_ref[...]
    return dot(high, basis) + dot(low, basis) + dot(high, low_ref[...])


def shares(rows):
    padded = -(-rows // 8) * 8
    direct = padded * 2 // 3 // 8 * 8
    middle = direct + (padded - direct) // 16 * 8
    return direct, ((direct, middle - direct), (middle, padded - middle))


def substep_kernel(
    sizes,
    depth_ref, kept_ref, slot_ref, coarse_ref, fine_ref,
    we_hbm, wn_hbm, th_hbm, geo_hbm, sg_hbm,
    east_hbm, north_hbm, thick_hbm, geo_new_hbm, spectra_hbm,
    we, wn, th, geo, sg, spectra_out, rows_ref, high_ref, low_ref, part, came,
    lon_put, lon_got, lat_put, lat_got, column_put, column_got, spec_put, spec_got, table_ref, hop_in, hop_over,
    in_sem, out_sem, lon_sem, lat_sem, part_sem, hop_sem, column_sem, spec_sem,
):
    lat_count, polar_bands, half_axis, nlon_total, phi_step, north_coef = sizes
    lev_dev, lat_dev, lon_dev = we.shape
    help_rows = spec_put.shape[1]
    lon = lax.axis_index("lon")
    lat = lax.axis_index("lat")
    lev = lax.axis_index("lev")
    east_out, north_out, thick_out, geo_out = we, wn, th, geo
    other_lon = {"lon": 1 - lon}
    other_lev = {"lev": 1 - lev}
    partner = lax.rem(lat + half_axis, lat_count)
    far = {"lat": partner}
    has_south = lat > 0
    has_north = lat < lat_count - 1
    polar = (lat < polar_bands) | (lat >= lat_count - polar_bands)
    MESH = pl.DeviceIdType.MESH

    loads = [
        pltpu.make_async_copy(src.at[:, level, :], dst.at[level], in_sem.at[i, level])
        for i, (src, dst) in enumerate(((geo_hbm, geo), (we_hbm, we), (wn_hbm, wn), (th_hbm, th)))
        for level in range(lev_dev)
    ]
    loads.append(pltpu.make_async_copy(sg_hbm, sg, in_sem.at[4, 0]))
    for load in loads:
        load.start()

    barrier = pltpu.get_barrier_semaphore()
    for target in (other_lon, other_lev, far):
        pl.semaphore_signal(barrier, inc=1, device_id=target, device_id_type=MESH)

    @pl.when(has_south)
    def _():
        pl.semaphore_signal(barrier, inc=1, device_id={"lat": lat - 1}, device_id_type=MESH)

    @pl.when(has_north)
    def _():
        pl.semaphore_signal(barrier, inc=1, device_id={"lat": lat + 1}, device_id_type=MESH)

    pl.semaphore_wait(barrier, 3 + has_south.astype(jnp.int32) + has_north.astype(jnp.int32))

    def remote(src, dst, sems, target):
        return pltpu.make_async_remote_copy(
            src_ref=src, dst_ref=dst, send_sem=sems.at[0], recv_sem=sems.at[1],
            device_id=target, device_id_type=MESH,
        )

    lane = lax.broadcasted_iota(jnp.int32, (lat_dev, lon_dev), 1)
    row = lax.broadcasted_iota(jnp.int32, (lat_dev, lon_dev), 0)
    edge_lane = lax.broadcasted_iota(jnp.int32, (lat_dev, 128), 1)

    def send_lon(turn, field):
        held = jnp.zeros((lat_dev, 128), jnp.float32)
        for level in range(lev_dev):
            held = jnp.where(edge_lane == 2 * level, field[level, :, 0:1], held)
            held = jnp.where(edge_lane == 2 * level + 1, field[level, :, lon_dev - 1 : lon_dev], held)
        lon_put[turn, :, 0:lat_dev] = jnp.transpose(held)[0:8]
        copy = remote(lon_put.at[turn], lon_got.at[turn], lon_sem.at[turn], other_lon)
        copy.start()
        return copy

    def send_lat(turn, field, scale):
        for level in range(lev_dev):
            lat_put[turn, 0, level : level + 1, :] = field[level, 0:1, :] * scale[0:1]
            lat_put[turn, 1, level : level + 1, :] = (
                field[level, lat_dev - 1 : lat_dev, :] * scale[lat_dev - 1 : lat_dev]
            )
        south = remote(lat_put.at[turn, 0], lat_got.at[turn, 1], lat_sem.at[turn, 0], {"lat": lat - 1})
        north = remote(lat_put.at[turn, 1], lat_got.at[turn, 0], lat_sem.at[turn, 1], {"lat": lat + 1})

        @pl.when(has_south)
        def _():
            south.start()

        @pl.when(has_north)
        def _():
            north.start()

        @pl.when(jnp.logical_not(has_south))
        def _():
            lat_got[turn, 0] = jnp.zeros_like(lat_got[turn, 0])

        @pl.when(jnp.logical_not(has_north))
        def _():
            lat_got[turn, 1] = jnp.zeros_like(lat_got[turn, 1])

        return south, north

    def wait_lat(south, north):
        @pl.when(has_south)
        def _():
            south.wait_send()
            north.wait_recv()

        @pl.when(has_north)
        def _():
            north.wait_send()
            south.wait_recv()

    def east_diff(x, turn, level, rims):
        first = rims[:, 2 * level : 2 * level + 1]
        last = rims[:, 2 * level + 1 : 2 * level + 2]
        up = jnp.where(lane == lon_dev - 1, first, pltpu.roll(x, lon_dev - 1, 1))
        down = jnp.where(lane == 0, last, pltpu.roll(x, 1, 1))
        return up - down

    def north_diff(x, turn, level):
        up = jnp.concatenate([x[1:], lat_got[turn, 1, level : level + 1, :]], axis=0)
        down = jnp.concatenate([lat_got[turn, 0, level : level + 1, :], x[:-1]], axis=0)
        return up - down

    row_id = lax.broadcasted_iota(jnp.int32, (lat_dev, 1), 0) + lat * lat_dev
    latitude = -0.5 * math.pi + (row_id.astype(jnp.float32) + 0.5) * phi_step
    cos_lat = jnp.cos(latitude)
    sin_lat = jnp.sin(latitude)
    east_coef = STEP_FACTOR / cos_lat
    flux_coef = north_coef / cos_lat
    one = jnp.ones((lat_dev, 1), jnp.float32)

    for load in loads[:lev_dev]:
        load.wait()
    lon_copy = send_lon(0, geo)
    lat_copies = send_lat(0, geo, one)

    def make_basis(block, _):
        p = coarse_ref[0, pl.ds(block, 1), :]
        q = coarse_ref[1, pl.ds(block, 1), :]
        values = p * fine_ref[0] + q * fine_ref[1]
        high, low = split(values)
        at = pl.ds(pl.multiple_of(block * FINE, FINE), FINE)
        high_ref[at, :] = high
        low_ref[at, :] = low
        return _

    @pl.when(polar)
    def _():
        lax.fori_loop(0, lon_dev // FINE, make_basis, 0)

    for load in loads[lev_dev:]:
        load.wait()
    lon_copy.wait()
    wait_lat(*lat_copies)

    rims = jnp.transpose(lon_got[0])[0:lat_dev]
    next_band = {"lat": lat + 1 - 2 * lax.rem(lat, 2)}
    rows = 2 * lat_dev
    direct, chunks = shares(rows)
    straight, hops = [], []
    for level in range(lev_dev):
        ahead = pl.ds(0, direct)
        straight.append(
            remote(part.at[level, ahead], came.at[level, ahead], part_sem.at[level], other_lon)
        )
        for chunk, (start, size) in enumerate(chunks):
            full, held = pl.ds(start, size), pl.ds(start - direct, size)
            hops.append(
                (
                    remote(part.at[level, full], hop_in.at[level, held], hop_sem.at[level, chunk, 0], next_band),
                    remote(hop_in.at[level, held], hop_over.at[level, held], hop_sem.at[level, chunk, 1], other_lon),
                    remote(hop_over.at[level, held], came.at[level, full], hop_sem.at[level, chunk, 2], next_band),
                )
            )
    for level in range(lev_dev):
        x = geo[level]
        east = we[level]
        north = wn[level]
        east_new = east - east_coef * east_diff(x, 0, level, rims) + CORIOLIS * sin_lat * north
        north_new = north - north_coef * north_diff(x, 0, level) - CORIOLIS * sin_lat * east
        east_out[level] = east_new
        north_out[level] = north_new

        @pl.when(polar)
        def _():
            rows_ref[level, 0:lat_dev, :] = east_new
            rows_ref[level, lat_dev:, :] = north_new
            part[level, 0:rows, :] = three_pass(rows_ref[level], high_ref, low_ref, ((1,), (0,)))
            for out, _, _ in hops[level * len(chunks) : (level + 1) * len(chunks)]:
                out.start()
            straight[level].start()

    @pl.when(jnp.logical_not(polar))
    def _():
        for out, over, _ in hops:
            out.wait_recv()
            over.start()
        for _, over, back in hops:
            over.wait_recv()
            back.start()
        for _, over, back in hops:
            over.wait_send()
            back.wait_send()

    column_id = lax.broadcasted_iota(jnp.int32, (lat_dev, 2 * KMAX), 1)
    wavenumber = jnp.where(column_id < KMAX, column_id, column_id - KMAX)
    weight = jnp.where(wavenumber == 0, 1.0 / nlon_total, 2.0 / nlon_total)
    odd = 1.0 - 2.0 * lax.rem(wavenumber, 2).astype(jnp.float32)
    first = jnp.where(lat < polar_bands, lat, jnp.maximum(lat - (lat_count - 2 * polar_bands), 0))
    first = jnp.minimum(first, 2 * polar_bands - 1)
    table_ref[...] = jnp.zeros_like(table_ref)
    for band in range(2 * polar_bands):
        columns = slice(band * lat_dev, (band + 1) * lat_dev)

        @pl.when(first == band)
        def _():
            table_ref[0:1, 0:lat_dev] = kept_ref[:, columns].astype(jnp.float32)
            table_ref[1:2, 0:lat_dev] = slot_ref[:, columns].astype(jnp.float32)

    table = jnp.transpose(table_ref[...])
    kept = table[0:lat_dev, 0:1].astype(jnp.int32)
    slots = table[0:lat_dev, 1:2].astype(jnp.int32)
    factor = jnp.where(wavenumber < kept, weight, 0.0)
    factor2 = jnp.concatenate([factor, factor], axis=0)
    odd_row = odd[0:1]

    @pl.when(polar)
    def _():
        for level in range(lev_dev):
            straight[level].wait()
            for out, _, back in hops[level * len(chunks) : (level + 1) * len(chunks)]:
                out.wait_send()
                back.wait_recv()
            kept_sums = (part[level, 0:rows, :] + odd_row * came[level, 0:rows, :]) * factor2
            part[level, 0:rows, :] = kept_sums
            filtered = three_pass(kept_sums, high_ref, low_ref, ((1,), (1,)))
            east_out[level] = filtered[0:lat_dev]
            north_out[level] = filtered[lat_dev:]

    lon_copy = send_lon(1, east_out)
    lat_copies = send_lat(1, north_out, cos_lat)
    stores = []

    def store(index, src, dst):
        for level in range(lev_dev):
            copy = pltpu.make_async_copy(src.at[level], dst.at[:, level, :], out_sem.at[index, level])
            copy.start()
            stores.append(copy)

    store(0, east_out, east_hbm)
    store(1, north_out, north_hbm)

    place = lax.broadcasted_iota(jnp.int32, (lat_dev, help_rows), 1)
    match_own = (slots == lat * help_rows + place).astype(jnp.float32)
    match_far = (slots == partner * help_rows + place).astype(jnp.float32)

    def gathered(match, level, wind):
        values = part[level, wind * lat_dev : (wind + 1) * lat_dev, :]
        picked = lax.dot_general(
            match, values, (((0,), (0,)), ((), ())),
            precision=lax.Precision.HIGHEST, preferred_element_type=jnp.float32,
        )
        spun = picked * odd[0:help_rows]
        return jnp.where(lon == 0, picked[:, 0:KMAX], spun[:, KMAX:])

    spec_copy = remote(spec_put, spec_got, spec_sem, far)

    @pl.when(polar)
    def _():
        for wind in range(2):
            for level in range(lev_dev):
                spec_put[wind * lev_dev + level] = gathered(match_far, level, wind)
        spec_copy.start()
        for wind in range(2):
            for level in range(lev_dev):
                spectra_out[wind, level] = gathered(match_own, level, wind)

    lon_copy.wait()
    wait_lat(*lat_copies)
    rims = jnp.transpose(lon_got[1])[0:lat_dev]
    below = None
    for level in range(lev_dev - 1, -1, -1):
        flux = north_out[level] * cos_lat
        divergence = east_coef * east_diff(east_out[level], 1, level, rims) + flux_coef * north_diff(
            flux, 1, level
        )
        thick = th[level] - depth_ref[level] * divergence
        thick_out[level] = thick
        below = thick if below is None else below + thick
        geo_out[level] = below
    store(2, thick_out, thick_hbm)
    column_put[...] = below
    column_copy = remote(column_put, column_got, column_sem, other_lev)

    @pl.when(lev == 1)
    def _():
        column_copy.start()
        for level in range(lev_dev):
            geo_out[level] = sg[...] + GRAVITY * geo_out[level]

    @pl.when(lev == 0)
    def _():
        column_copy.wait_recv()
        for level in range(lev_dev):
            geo_out[level] = sg[...] + GRAVITY * (geo_out[level] + column_got[...])

    store(3, geo_out, geo_new_hbm)

    @pl.when(lev == 1)
    def _():
        column_copy.wait_send()

    @pl.when(polar)
    def _():
        spec_copy.wait_send()

    @pl.when(jnp.logical_not(polar))
    def _():
        spec_copy.wait_recv()
        for wind in range(2):
            for level in range(lev_dev):
                spectra_out[wind, level] = spec_got[wind * lev_dev + level]

    for wind in range(2):
        for level in range(lev_dev):
            copy = pltpu.make_async_copy(
                spectra_out.at[wind, level],
                spectra_hbm.at[wind, :, level, :],
                out_sem.at[4, wind * lev_dev + level],
            )
            copy.start()
            stores.append(copy)
    for copy in stores:
        copy.wait()


def one_kernel(
    wind_east, wind_north, thickness, geopot, surface_geopot, mean_depth, kept_modes, slot_table
):
    lev_dev, lat_dev, lon_dev = thickness.shape
    lat_count = lax.axis_size("lat")
    nlat_total = lat_dev * lat_count
    nlon_total = 2 * lon_dev
    help_rows = lat_dev // 2
    lam_step = 2.0 * math.pi / nlon_total
    phi_step = math.pi / nlat_total
    north_coef = STEP_FACTOR * lam_step / phi_step
    coarse, fine = angle_tables(lon_dev, nlon_total)
    whole = pl.BlockSpec(memory_space=pltpu.VMEM)
    away = pl.BlockSpec(memory_space=pl.ANY)
    field = jax.ShapeDtypeStruct((lat_dev, lev_dev, lon_dev), jnp.float32)
    block = pltpu.VMEM((lev_dev, lat_dev, lon_dev), jnp.float32)
    basis = pltpu.VMEM((lon_dev, 2 * KMAX), jnp.bfloat16)
    padded_rows = -(-2 * lat_dev // 8) * 8
    sums = pltpu.VMEM((lev_dev, padded_rows, 2 * KMAX), jnp.float32)
    specs = pltpu.VMEM((2 * lev_dev, help_rows, KMAX), jnp.float32)
    dma = pltpu.SemaphoreType.DMA
    direct, chunks = shares(2 * lat_dev)
    hop = pltpu.VMEM((lev_dev, padded_rows - direct, 2 * KMAX), jnp.float32)
    *fields, spectra = pl.pallas_call(
        functools.partial(
            substep_kernel,
            (lat_count, lat_count // 4, lat_count // 2, nlon_total, phi_step, north_coef),
        ),
        out_shape=(field,) * 4
        + (jax.ShapeDtypeStruct((2, help_rows, lev_dev, KMAX), jnp.float32),),
        in_specs=[pl.BlockSpec(memory_space=pltpu.SMEM)] + [whole] * 4 + [away] * 5,
        out_specs=(away,) * 5,
        scratch_shapes=[
            block, block, block, block,
            pltpu.VMEM((lat_dev, lon_dev), jnp.float32),
            pltpu.VMEM((2, lev_dev, help_rows, KMAX), jnp.float32),
            pltpu.VMEM((lev_dev, 2 * lat_dev, lon_dev), jnp.float32),
            basis, basis, sums, sums,
            pltpu.VMEM((2, 8, 128), jnp.float32),
            pltpu.VMEM((2, 8, 128), jnp.float32),
            pltpu.VMEM((2, 2, lev_dev, lon_dev), jnp.float32),
            pltpu.VMEM((2, 2, lev_dev, lon_dev), jnp.float32),
            pltpu.VMEM((lat_dev, lon_dev), jnp.float32),
            pltpu.VMEM((lat_dev, lon_dev), jnp.float32),
            specs, specs,
            pltpu.VMEM((8, 128), jnp.float32), hop, hop,
            dma((5, lev_dev)), dma((5, 2 * lev_dev)), dma((2, 2)), dma((2, 2, 2)), dma((lev_dev, 2)), dma((lev_dev, len(chunks), 3, 2)), dma((2,)), dma((2,)),
        ],
        compiler_params=pltpu.CompilerParams(
            collective_id=0, has_side_effects=True, vmem_limit_bytes=60 * 2**20
        ),
    )(
        mean_depth,
        kept_modes.reshape(1, -1),
        slot_table.reshape(1, -1),
        jnp.asarray(coarse),
        jnp.asarray(fine),
        *(jnp.transpose(x, (1, 0, 2)) for x in (wind_east, wind_north, thickness, geopot)),
        surface_geopot,
    )
    return (*(jnp.transpose(x, (1, 0, 2)) for x in fields), jnp.transpose(spectra, (0, 2, 1, 3)))


def solution(mesh):
    body = one_kernel if dict(mesh.shape, members=2) == dict(members=2, lat=4, lon=2, lev=2) else local
    return jax.shard_map(
        body,
        mesh=mesh,
        in_specs=(
            P(("members", "lev"), "lat", "lon"),
            P(("members", "lev"), "lat", "lon"),
            P(("members", "lev"), "lat", "lon"),
            P(("members", "lev"), "lat", "lon"),
            P("lat", "lon"),
            P("lev"),
            P(),
            P(),
        ),
        out_specs=(
            P(("members", "lev"), "lat", "lon"),
            P(("members", "lev"), "lat", "lon"),
            P(("members", "lev"), "lat", "lon"),
            P(("members", "lev"), "lat", "lon"),
            P(None, ("members", "lev"), "lat", "lon"),
        ),
        check_vma=False,
    )
```

```python
import math

import functools

import jax
import numpy as np
import jax.numpy as jnp
from jax import lax
from jax.experimental import pallas as pl
from jax.experimental.pallas import tpu as pltpu
from jax.sharding import PartitionSpec as P

KMAX = 360


STEP_FACTOR = 0.15
CORIOLIS = 0.2
GRAVITY = 0.25


def edges(block, axis, dim, periodic):
    count = lax.axis_size(axis)
    first = lax.slice_in_dim(block, 0, 1, axis=dim)
    last = lax.slice_in_dim(block, block.shape[dim] - 1, block.shape[dim], axis=dim)
    if periodic and count == 2:
        both = lax.ppermute(jnp.concatenate([last, first], axis=dim), axis, [(0, 1), (1, 0)])
        return lax.slice_in_dim(both, 0, 1, axis=dim), lax.slice_in_dim(both, 1, 2, axis=dim)
    forward = [(i, i + 1) for i in range(count - 1)]
    if periodic:
        forward.append((count - 1, 0))
    backward = [(target, source) for source, target in forward]
    return lax.ppermute(last, axis, forward), lax.ppermute(first, axis, backward)


def diff(block, low, high, dim):
    size = block.shape[dim]
    up = jnp.concatenate([lax.slice_in_dim(block, 1, size, axis=dim), high], axis=dim)
    down = jnp.concatenate([low, lax.slice_in_dim(block, 0, size - 1, axis=dim)], axis=dim)
    return up - down


def local_basis(count, nlon_total):
    fine = next(f for f in (24, 20, 18, 16, 12, 8, 6, 5, 4, 3, 2, 1) if count % f == 0)
    k = np.arange(KMAX, dtype=np.int64)[None, :]
    angle = 2.0 * np.pi / nlon_total

    def table(columns):
        phase = (columns[:, None] * k % nlon_total) * angle
        return np.cos(phase).astype(np.float32), np.sin(phase).astype(np.float32)

    cc, cs = (jnp.asarray(t)[:, None] for t in table(np.arange(0, count, fine)))
    fc, fs = (jnp.asarray(t)[None] for t in table(np.arange(fine)))
    return (
        (cc * fc - cs * fs).reshape(count, KMAX),
        (cs * fc + cc * fs).reshape(count, KMAX),
    )


def turned(pair, cos_shift, sin_shift):
    cos_part, sin_part = pair[..., :KMAX], pair[..., KMAX:]
    return jnp.concatenate(
        [cos_shift * cos_part - sin_shift * sin_part, sin_shift * cos_part + cos_shift * sin_part],
        axis=-1,
    )


def local(
    wind_east, wind_north, thickness, geopot, surface_geopot, mean_depth, kept_modes, slot_table
):
    lev_dev, lat_dev, lon_dev = thickness.shape
    lat_count = lax.axis_size("lat")
    lon_count = lax.axis_size("lon")
    lev_count = lax.axis_size("lev")
    lat_index = lax.axis_index("lat")
    lon_index = lax.axis_index("lon")
    nlat_total = lat_dev * lat_count
    nlon_total = lon_dev * lon_count
    polar_count = nlat_total // 4
    slot_count = 2 * polar_count
    help_rows = lat_dev // 2
    half_axis = lat_count // 2
    lam_step = 2.0 * math.pi / nlon_total
    phi_step = math.pi / nlat_total
    global_rows = lat_index * lat_dev + jnp.arange(lat_dev, dtype=jnp.int32)
    latitude = -0.5 * math.pi + (global_rows.astype(jnp.float32) + 0.5) * phi_step
    coslat = jnp.cos(latitude)[:, None]
    sinlat = jnp.sin(latitude)[:, None]
    east_coef = STEP_FACTOR / coslat
    north_coef = STEP_FACTOR * lam_step / phi_step
    geo_west, geo_east = edges(geopot, "lon", 2, True)
    geo_south, geo_north = edges(geopot, "lat", 1, False)
    east_new = (
        wind_east
        - east_coef * diff(geopot, geo_west, geo_east, 2)
        + CORIOLIS * sinlat * wind_north
    )
    north_new = (
        wind_north
        - north_coef * diff(geopot, geo_south, geo_north, 1)
        - CORIOLIS * sinlat * wind_east
    )
    is_polar = (lat_index < lat_count // 4) | (lat_index >= lat_count - lat_count // 4)
    first_row = lat_index * lat_dev
    first_rank = jnp.where(lat_index < lat_count // 4, first_row, first_row - (nlat_total - slot_count))
    first_rank = jnp.clip(first_rank, 0, slot_count - lat_dev)
    kept = lax.dynamic_slice(kept_modes, (first_rank,), (lat_dev,))
    slots = lax.dynamic_slice(slot_table, (first_rank,), (lat_dev,))
    wavenumber = jnp.arange(2 * KMAX, dtype=jnp.int32) % KMAX
    weight = (jnp.where(wavenumber == 0, 1.0, 2.0) / nlon_total).astype(jnp.float32)
    factor = jnp.where(wavenumber[None, :] < kept[:, None], weight[None, :], 0.0)
    cos_basis, sin_basis = local_basis(lon_dev, nlon_total)
    basis = jnp.concatenate([cos_basis, sin_basis], axis=1)
    shift = (lon_index * jnp.arange(KMAX, dtype=jnp.int32) % lon_count).astype(jnp.float32)
    shift = shift * (2.0 * math.pi / lon_count)
    if lon_count == 2:
        cos_shift = 1.0 - 2.0 * (lon_index * jnp.arange(KMAX, dtype=jnp.int32) % 2).astype(jnp.float32)
        sin_shift = jnp.zeros_like(cos_shift)
    else:
        cos_shift, sin_shift = jnp.cos(shift), jnp.sin(shift)
    pieces = [wind[level] for level in range(lev_dev) for wind in (east_new, north_new)]
    both_sums = []
    for piece in range(lev_dev):
        rows = jnp.concatenate(pieces[2 * piece : 2 * piece + 2], axis=0)
        part = jnp.dot(rows, basis, precision=lax.Precision.HIGH)
        part = turned(part, cos_shift, sin_shift)
        if lon_count == 2:
            sums = part + lax.ppermute(part, "lon", [(0, 1), (1, 0)])
        else:
            sums = lax.psum(part, "lon")
        both_sums.append(sums.reshape(2, lat_dev, 2 * KMAX) * factor[None])
    filtered = []
    for sums in both_sums:
        turned_back = turned(sums, cos_shift, -sin_shift)
        rows = lax.dot_general(
            turned_back.reshape(2 * lat_dev, 2 * KMAX),
            basis,
            (((1,), (1,)), ((), ())),
            precision=lax.Precision.HIGH,
        )
        filtered.append(rows.reshape(2, lat_dev, lon_dev))
    filtered = jnp.stack(filtered, axis=1)
    east_final = jnp.where(is_polar, filtered[0], east_new)
    north_final = jnp.where(is_polar, filtered[1], north_new)

    slice_width = 2 * KMAX // lon_count
    kept_sums = jnp.stack(both_sums, axis=1)
    own = lax.dynamic_slice_in_dim(kept_sums, lon_index * slice_width, slice_width, 3)
    places = jnp.arange(help_rows, dtype=jnp.int32)
    partner = (lat_index + half_axis) % lat_count

    def rows_named(device):
        match = slots[None, :] == (device * help_rows + places)[:, None]
        return jnp.einsum(
            "sr,abrc->absc", match.astype(jnp.float32), own, precision=lax.Precision.HIGHEST
        )

    route = [((i - half_axis) % lat_count, i) for i in range(lat_count)]
    route = [(s, t) for s, t in route if s < lat_count // 4 or s >= lat_count - lat_count // 4]
    arrived = lax.ppermute(rows_named(partner), "lat", route)
    spectra = jnp.where(is_polar, rows_named(lat_index), arrived)

    rim_west, rim_east = edges(east_final, "lon", 2, True)
    flux = north_final * coslat
    rim_south, rim_north = edges(flux, "lat", 1, False)
    divergence = east_coef * diff(east_final, rim_west, rim_east, 2) + north_coef / coslat * diff(
        flux, rim_south, rim_north, 1
    )
    thick_new = thickness - mean_depth[:, None, None] * divergence
    columns = [thick_new[lev_dev - 1]]
    for level in range(lev_dev - 2, -1, -1):
        columns.append(columns[-1] + thick_new[level])
    columns = columns[::-1]
    deeper = jnp.zeros_like(columns[0])
    for distance in range(1, lev_count):
        deeper = deeper + lax.ppermute(
            columns[0], "lev", [(i + distance, i) for i in range(lev_count - distance)]
        )
    geo_new = surface_geopot[None] + GRAVITY * (jnp.stack(columns) + deeper[None])
    return (east_final, north_final, thick_new, geo_new, spectra)


FINE = 32
VMEM_MIB = 60
STEPS = 5


def angle_tables(count, nlon_total):
    k = np.arange(KMAX, dtype=np.int64)[None, :]
    angle = 2.0 * np.pi / nlon_total

    def table(columns):
        phase = (columns[:, None] * k % nlon_total) * angle
        return np.cos(phase), np.sin(phase)

    cc, cs = table(np.arange(0, count, FINE))
    fc, fs = table(np.arange(FINE))
    coarse = np.stack([np.concatenate([cc, cs], 1), np.concatenate([-cs, cc], 1)])
    fine = np.stack([np.concatenate([fc, fc], 1), np.concatenate([fs, fs], 1)])
    return coarse.astype(np.float32), fine.astype(np.float32)


def split(x):
    high = x.astype(jnp.bfloat16)
    return high, (x - high.astype(jnp.float32)).astype(jnp.bfloat16)


def three_pass(x, high_ref, low_ref, dims):
    high, low = split(x)
    rows = x.shape[0]

    def dot(a, b):
        return lax.dot_general(a, b, (dims, ((), ())), preferred_element_type=jnp.float32)

    basis = high_ref[...]
    return dot(high, basis) + dot(low, basis) + dot(high, low_ref[...])


def shares(rows):
    padded = -(-rows // 8) * 8
    direct = padded * 2 // 3 // 8 * 8
    middle = direct + (padded - direct) // 16 * 8
    return direct, ((direct, middle - direct), (middle, padded - middle))


def substep_kernel(
    sizes,
    depth_ref, kept_ref, slot_ref, coarse_ref, fine_ref,
    we_hbm, wn_hbm, th_hbm, geo_hbm, sg_hbm,
    east_hbm, north_hbm, thick_hbm, geo_new_hbm, spectra_hbm,
    we, wn, th, geo, sg, spectra_out, rows_ref, high_ref, low_ref, part, came,
    lon_put, lon_got, lat_put, lat_got, column_put, column_got, spec_put, spec_got, table_ref, hop_in, hop_over,
    in_sem, out_sem, lon_sem, lat_sem, part_sem, hop_sem, column_sem, spec_sem,
):
    lat_count, polar_bands, half_axis, nlon_total, phi_step, north_coef = sizes
    lev_dev, lat_dev, lon_dev = we.shape
    help_rows = spec_put.shape[1]
    lon = lax.axis_index("lon")
    lat = lax.axis_index("lat")
    lev = lax.axis_index("lev")
    east_out, north_out, thick_out, geo_out = we, wn, th, geo
    other_lon = {"lon": 1 - lon}
    other_lev = {"lev": 1 - lev}
    partner = lax.rem(lat + half_axis, lat_count)
    far = {"lat": partner}
    has_south = lat > 0
    has_north = lat < lat_count - 1
    polar = (lat < polar_bands) | (lat >= lat_count - polar_bands)
    MESH = pl.DeviceIdType.MESH

    loads = [
        pltpu.make_async_copy(src.at[:, level, :], dst.at[level], in_sem.at[i, level])
        for i, (src, dst) in enumerate(((geo_hbm, geo), (we_hbm, we), (wn_hbm, wn), (th_hbm, th)))
        for level in range(lev_dev)
    ]
    loads.append(pltpu.make_async_copy(sg_hbm, sg, in_sem.at[4, 0]))
    for load in loads:
        load.start()

    barrier = pltpu.get_barrier_semaphore()
    for target in (other_lon, other_lev, far):
        pl.semaphore_signal(barrier, inc=1, device_id=target, device_id_type=MESH)

    @pl.when(has_south)
    def _():
        pl.semaphore_signal(barrier, inc=1, device_id={"lat": lat - 1}, device_id_type=MESH)

    @pl.when(has_north)
    def _():
        pl.semaphore_signal(barrier, inc=1, device_id={"lat": lat + 1}, device_id_type=MESH)

    pl.semaphore_wait(barrier, 3 + has_south.astype(jnp.int32) + has_north.astype(jnp.int32))

    def remote(src, dst, sems, target):
        return pltpu.make_async_remote_copy(
            src_ref=src, dst_ref=dst, send_sem=sems.at[0], recv_sem=sems.at[1],
            device_id=target, device_id_type=MESH,
        )

    lane = lax.broadcasted_iota(jnp.int32, (lat_dev, lon_dev), 1)
    row = lax.broadcasted_iota(jnp.int32, (lat_dev, lon_dev), 0)
    edge_lane = lax.broadcasted_iota(jnp.int32, (lat_dev, 128), 1)

    def send_lon(turn, field):
        held = jnp.zeros((lat_dev, 128), jnp.float32)
        for level in range(lev_dev):
            held = jnp.where(edge_lane == 2 * level, field[level, :, 0:1], held)
            held = jnp.where(edge_lane == 2 * level + 1, field[level, :, lon_dev - 1 : lon_dev], held)
        lon_put[turn, :, 0:lat_dev] = jnp.transpose(held)[0:8]
        copy = remote(lon_put.at[turn], lon_got.at[turn], lon_sem.at[turn], other_lon)
        copy.start()
        return copy

    def send_lat(turn, field, scale):
        for level in range(lev_dev):
            lat_put[turn, 0, level : level + 1, :] = field[level, 0:1, :] * scale[0:1]
            lat_put[turn, 1, level : level + 1, :] = (
                field[level, lat_dev - 1 : lat_dev, :] * scale[lat_dev - 1 : lat_dev]
            )
        south = remote(lat_put.at[turn, 0], lat_got.at[turn, 1], lat_sem.at[turn, 0], {"lat": lat - 1})
        north = remote(lat_put.at[turn, 1], lat_got.at[turn, 0], lat_sem.at[turn, 1], {"lat": lat + 1})

        @pl.when(has_south)
        def _():
            south.start()

        @pl.when(has_north)
        def _():
            north.start()

        @pl.when(jnp.logical_not(has_south))
        def _():
            lat_got[turn, 0] = jnp.zeros_like(lat_got[turn, 0])

        @pl.when(jnp.logical_not(has_north))
        def _():
            lat_got[turn, 1] = jnp.zeros_like(lat_got[turn, 1])

        return south, north

    def wait_lat(south, north):
        @pl.when(has_south)
        def _():
            south.wait_send()
            north.wait_recv()

        @pl.when(has_north)
        def _():
            north.wait_send()
            south.wait_recv()

    def east_diff(x, turn, level, rims):
        first = rims[:, 2 * level : 2 * level + 1]
        last = rims[:, 2 * level + 1 : 2 * level + 2]
        up = jnp.where(lane == lon_dev - 1, first, pltpu.roll(x, lon_dev - 1, 1))
        down = jnp.where(lane == 0, last, pltpu.roll(x, 1, 1))
        return up - down

    def north_diff(x, turn, level):
        up = jnp.concatenate([x[1:], lat_got[turn, 1, level : level + 1, :]], axis=0)
        down = jnp.concatenate([lat_got[turn, 0, level : level + 1, :], x[:-1]], axis=0)
        return up - down

    row_id = lax.broadcasted_iota(jnp.int32, (lat_dev, 1), 0) + lat * lat_dev
    latitude = -0.5 * math.pi + (row_id.astype(jnp.float32) + 0.5) * phi_step
    cos_lat = jnp.cos(latitude)
    sin_lat = jnp.sin(latitude)
    east_coef = STEP_FACTOR / cos_lat
    flux_coef = north_coef / cos_lat
    one = jnp.ones((lat_dev, 1), jnp.float32)

    for load in loads[:lev_dev]:
        load.wait()
    lon_copy = send_lon(0, geo)
    lat_copies = send_lat(0, geo, one)

    def make_basis(block, _):
        p = coarse_ref[0, pl.ds(block, 1), :]
        q = coarse_ref[1, pl.ds(block, 1), :]
        values = p * fine_ref[0] + q * fine_ref[1]
        high, low = split(values)
        at = pl.ds(pl.multiple_of(block * FINE, FINE), FINE)
        high_ref[at, :] = high
        low_ref[at, :] = low
        return _

    @pl.when(polar)
    def _():
        lax.fori_loop(0, lon_dev // FINE, make_basis, 0)

    for load in loads[lev_dev:]:
        load.wait()
    lon_copy.wait()
    wait_lat(*lat_copies)

    rims = jnp.transpose(lon_got[0])[0:lat_dev]
    next_band = {"lat": lat + 1 - 2 * lax.rem(lat, 2)}
    rows = 2 * lat_dev
    direct, chunks = shares(rows)
    straight, hops = [], []
    for level in range(lev_dev):
        ahead = pl.ds(0, direct)
        straight.append(
            remote(part.at[level, ahead], came.at[level, ahead], part_sem.at[level], other_lon)
        )
        for chunk, (start, size) in enumerate(chunks):
            full, held = pl.ds(start, size), pl.ds(start - direct, size)
            hops.append(
                (
                    remote(part.at[level, full], hop_in.at[level, held], hop_sem.at[level, chunk, 0], next_band),
                    remote(hop_in.at[level, held], hop_over.at[level, held], hop_sem.at[level, chunk, 1], other_lon),
                    remote(hop_over.at[level, held], came.at[level, full], hop_sem.at[level, chunk, 2], next_band),
                )
            )
    for level in range(lev_dev):
        x = geo[level]
        east = we[level]
        north = wn[level]
        east_new = east - east_coef * east_diff(x, 0, level, rims) + CORIOLIS * sin_lat * north
        north_new = north - north_coef * north_diff(x, 0, level) - CORIOLIS * sin_lat * east
        east_out[level] = east_new
        north_out[level] = north_new

        @pl.when(polar)
        def _():
            rows_ref[level, 0:lat_dev, :] = east_new
            rows_ref[level, lat_dev:, :] = north_new
            part[level, 0:rows, :] = three_pass(rows_ref[level], high_ref, low_ref, ((1,), (0,)))
            for out, _, _ in hops[level * len(chunks) : (level + 1) * len(chunks)]:
                out.start()
            straight[level].start()

    @pl.when(jnp.logical_not(polar))
    def _():
        for out, over, _ in hops:
            out.wait_recv()
            over.start()
        for _, over, back in hops:
            over.wait_recv()
            back.start()
        for _, over, back in hops:
            over.wait_send()
            back.wait_send()

    column_id = lax.broadcasted_iota(jnp.int32, (lat_dev, 2 * KMAX), 1)
    wavenumber = jnp.where(column_id < KMAX, column_id, column_id - KMAX)
    weight = jnp.where(wavenumber == 0, 1.0 / nlon_total, 2.0 / nlon_total)
    odd = 1.0 - 2.0 * lax.rem(wavenumber, 2).astype(jnp.float32)
    first = jnp.where(lat < polar_bands, lat, jnp.maximum(lat - (lat_count - 2 * polar_bands), 0))
    first = jnp.minimum(first, 2 * polar_bands - 1)
    table_ref[...] = jnp.zeros_like(table_ref)
    for band in range(2 * polar_bands):
        columns = slice(band * lat_dev, (band + 1) * lat_dev)

        @pl.when(first == band)
        def _():
            table_ref[0:1, 0:lat_dev] = kept_ref[:, columns].astype(jnp.float32)
            table_ref[1:2, 0:lat_dev] = slot_ref[:, columns].astype(jnp.float32)

    table = jnp.transpose(table_ref[...])
    kept = table[0:lat_dev, 0:1].astype(jnp.int32)
    slots = table[0:lat_dev, 1:2].astype(jnp.int32)
    factor = jnp.where(wavenumber < kept, weight, 0.0)
    factor2 = jnp.concatenate([factor, factor], axis=0)
    odd_row = odd[0:1]

    @pl.when(polar)
    def _():
        for level in range(lev_dev):
            straight[level].wait()
            for out, _, back in hops[level * len(chunks) : (level + 1) * len(chunks)]:
                out.wait_send()
                back.wait_recv()
            kept_sums = (part[level, 0:rows, :] + odd_row * came[level, 0:rows, :]) * factor2
            part[level, 0:rows, :] = kept_sums
            filtered = three_pass(kept_sums, high_ref, low_ref, ((1,), (1,)))
            east_out[level] = filtered[0:lat_dev]
            north_out[level] = filtered[lat_dev:]

    lon_copy = send_lon(1, east_out)
    lat_copies = send_lat(1, north_out, cos_lat)
    stores = []

    def store(index, src, dst):
        for level in range(lev_dev):
            copy = pltpu.make_async_copy(src.at[level], dst.at[:, level, :], out_sem.at[index, level])
            copy.start()
            stores.append(copy)

    store(0, east_out, east_hbm)
    store(1, north_out, north_hbm)

    place = lax.broadcasted_iota(jnp.int32, (lat_dev, help_rows), 1)
    match_own = (slots == lat * help_rows + place).astype(jnp.float32)
    match_far = (slots == partner * help_rows + place).astype(jnp.float32)

    def gathered(match, level, wind):
        values = part[level, wind * lat_dev : (wind + 1) * lat_dev, :]
        picked = lax.dot_general(
            match, values, (((0,), (0,)), ((), ())),
            precision=lax.Precision.HIGHEST, preferred_element_type=jnp.float32,
        )
        spun = picked * odd[0:help_rows]
        return jnp.where(lon == 0, picked[:, 0:KMAX], spun[:, KMAX:])

    spec_copy = remote(spec_put, spec_got, spec_sem, far)

    @pl.when(polar)
    def _():
        for wind in range(2):
            for level in range(lev_dev):
                spec_put[wind * lev_dev + level] = gathered(match_far, level, wind)
        spec_copy.start()
        for wind in range(2):
            for level in range(lev_dev):
                spectra_out[wind, level] = gathered(match_own, level, wind)

    lon_copy.wait()
    wait_lat(*lat_copies)
    rims = jnp.transpose(lon_got[1])[0:lat_dev]
    below = None
    for level in range(lev_dev - 1, -1, -1):
        flux = north_out[level] * cos_lat
        divergence = east_coef * east_diff(east_out[level], 1, level, rims) + flux_coef * north_diff(
            flux, 1, level
        )
        thick = th[level] - depth_ref[level] * divergence
        thick_out[level] = thick
        below = thick if below is None else below + thick
        geo_out[level] = below
    store(2, thick_out, thick_hbm)
    column_put[...] = below
    column_copy = remote(column_put, column_got, column_sem, other_lev)

    @pl.when(lev == 1)
    def _():
        column_copy.start()
        for level in range(lev_dev):
            geo_out[level] = sg[...] + GRAVITY * geo_out[level]

    @pl.when(lev == 0)
    def _():
        column_copy.wait_recv()
        for level in range(lev_dev):
            geo_out[level] = sg[...] + GRAVITY * (geo_out[level] + column_got[...])

    store(3, geo_out, geo_new_hbm)

    @pl.when(lev == 1)
    def _():
        column_copy.wait_send()

    @pl.when(polar)
    def _():
        spec_copy.wait_send()

    @pl.when(jnp.logical_not(polar))
    def _():
        spec_copy.wait_recv()
        for wind in range(2):
            for level in range(lev_dev):
                spectra_out[wind, level] = spec_got[wind * lev_dev + level]

    for wind in range(2):
        for level in range(lev_dev):
            copy = pltpu.make_async_copy(
                spectra_out.at[wind, level],
                spectra_hbm.at[wind, :, level, :],
                out_sem.at[4, wind * lev_dev + level],
            )
            copy.start()
            stores.append(copy)
    for copy in stores:
        copy.wait()


def hand_on_kernel(*refs):
    half = len(refs) // 2
    for src, dst in zip(refs[:half], refs[half:]):
        dst[...] = src[...]


def handed_on(held):
    def spec(x):
        if x.ndim == 3:
            return pl.BlockSpec((x.shape[0] // STEPS, *x.shape[1:]), lambda i: (i, 0, 0))
        return pl.BlockSpec((x.shape[0], x.shape[1] // STEPS, *x.shape[2:]), lambda i: (0, i, 0, 0))

    specs = [spec(x) for x in held]
    return pl.pallas_call(
        hand_on_kernel,
        grid=(STEPS,),
        out_shape=[jax.ShapeDtypeStruct(x.shape, x.dtype) for x in held],
        in_specs=specs,
        out_specs=specs,
    )(*held)


def one_kernel(
    wind_east, wind_north, thickness, geopot, surface_geopot, mean_depth, kept_modes, slot_table
):
    lev_dev, lat_dev, lon_dev = thickness.shape
    lat_count = lax.axis_size("lat")
    nlat_total = lat_dev * lat_count
    nlon_total = 2 * lon_dev
    help_rows = lat_dev // 2
    lam_step = 2.0 * math.pi / nlon_total
    phi_step = math.pi / nlat_total
    north_coef = STEP_FACTOR * lam_step / phi_step
    coarse, fine = angle_tables(lon_dev, nlon_total)
    whole = pl.BlockSpec(memory_space=pltpu.VMEM)
    away = pl.BlockSpec(memory_space=pl.ANY)
    field = jax.ShapeDtypeStruct((lat_dev, lev_dev, lon_dev), jnp.float32)
    block = pltpu.VMEM((lev_dev, lat_dev, lon_dev), jnp.float32)
    basis = pltpu.VMEM((lon_dev, 2 * KMAX), jnp.bfloat16)
    padded_rows = -(-2 * lat_dev // 8) * 8
    sums = pltpu.VMEM((lev_dev, padded_rows, 2 * KMAX), jnp.float32)
    specs = pltpu.VMEM((2 * lev_dev, help_rows, KMAX), jnp.float32)
    dma = pltpu.SemaphoreType.DMA
    direct, chunks = shares(2 * lat_dev)
    hop = pltpu.VMEM((lev_dev, padded_rows - direct, 2 * KMAX), jnp.float32)
    held = pl.pallas_call(
        functools.partial(
            substep_kernel,
            (lat_count, lat_count // 4, lat_count // 2, nlon_total, phi_step, north_coef),
        ),
        out_shape=(field,) * 4
        + (jax.ShapeDtypeStruct((2, help_rows, lev_dev, KMAX), jnp.float32),),
        in_specs=[pl.BlockSpec(memory_space=pltpu.SMEM)] + [whole] * 4 + [away] * 5,
        out_specs=(away,) * 5,
        scratch_shapes=[
            block, block, block, block,
            pltpu.VMEM((lat_dev, lon_dev), jnp.float32),
            pltpu.VMEM((2, lev_dev, help_rows, KMAX), jnp.float32),
            pltpu.VMEM((lev_dev, 2 * lat_dev, lon_dev), jnp.float32),
            basis, basis, sums, sums,
            pltpu.VMEM((2, 8, 128), jnp.float32),
            pltpu.VMEM((2, 8, 128), jnp.float32),
            pltpu.VMEM((2, 2, lev_dev, lon_dev), jnp.float32),
            pltpu.VMEM((2, 2, lev_dev, lon_dev), jnp.float32),
            pltpu.VMEM((lat_dev, lon_dev), jnp.float32),
            pltpu.VMEM((lat_dev, lon_dev), jnp.float32),
            specs, specs,
            pltpu.VMEM((8, 128), jnp.float32), hop, hop,
            dma((5, lev_dev)), dma((5, 2 * lev_dev)), dma((2, 2)), dma((2, 2, 2)), dma((lev_dev, 2)), dma((lev_dev, len(chunks), 3, 2)), dma((2,)), dma((2,)),
        ],
        compiler_params=pltpu.CompilerParams(
            collective_id=0, has_side_effects=True, vmem_limit_bytes=VMEM_MIB * 2**20
        ),
    )(
        mean_depth,
        kept_modes.reshape(1, -1),
        slot_table.reshape(1, -1),
        jnp.asarray(coarse),
        jnp.asarray(fine),
        *(jnp.transpose(x, (1, 0, 2)) for x in (wind_east, wind_north, thickness, geopot)),
        surface_geopot,
    )
    *fields, spectra = handed_on(held)
    return (*(jnp.transpose(x, (1, 0, 2)) for x in fields), jnp.transpose(spectra, (0, 2, 1, 3)))


def solution(mesh):
    body = one_kernel if dict(mesh.shape, members=2) == dict(members=2, lat=4, lon=2, lev=2) else local
    return jax.shard_map(
        body,
        mesh=mesh,
        in_specs=(
            P(("members", "lev"), "lat", "lon"),
            P(("members", "lev"), "lat", "lon"),
            P(("members", "lev"), "lat", "lon"),
            P(("members", "lev"), "lat", "lon"),
            P("lat", "lon"),
            P("lev"),
            P(),
            P(),
        ),
        out_specs=(
            P(("members", "lev"), "lat", "lon"),
            P(("members", "lev"), "lat", "lon"),
            P(("members", "lev"), "lat", "lon"),
            P(("members", "lev"), "lat", "lon"),
            P(None, ("members", "lev"), "lat", "lon"),
        ),
        check_vma=False,
    )
```
